32 devices in a mesh: ctx: 8 (over z, y), grp: 4 (over x, core).
Axes of the slice: x: 2, y: 2, z: 4, core: 2. Of those that a mesh axis runs over, the one named last changes fastest.
Arguments:
- tokens: bfloat16 [4, 512, 8192], P('grp', 'ctx'), may hold values from -6 to 6
- queries: bfloat16 [4, 512, 4096], P('grp', 'ctx'), may hold values from -32 to 32
- key_value_weight: bfloat16 [8192, 1024], P('grp'), may hold values from -0.0625 to 0.0625
- adapter_down_weight: bfloat16 [8192, 128], P('grp'), may hold values from -0.0625 to 0.0625
- adapter_up_weight: bfloat16 [2, 64, 512], replicated, may hold values from -0.75 to 0.75
- tile_request_mask: int32 [4, 4, 4], P('grp'), may hold values 0 or 1
- lengths: int32 [4], P('grp'), may hold values from 128 to 512, as said below
- page_lookup_table: int32 [4, 128], P(None, 'ctx'), may hold values from 0 to 63, as said below
Outputs:
- attended: bfloat16 [4, 512, 4096], P('grp', 'ctx')
- decode_cache: bfloat16 [4, 128, 4, 1024], P('grp', 'ctx')
The draws below stay inside these ranges and needn't reach their ends.
Inputs may be any that keep to these rules, and one draw needn't show every extreme that they name: `page_lookup_table`: pages of positions held by one index of ctx go to decode-cache rows of that same index. Every decode group receives exactly 16 pages into distinct slots from the pages of each index of ctx. From the pages of one rollout on one index of ctx, at most max(2, ceil(4)) go to one group, and exactly that many to some group. `lengths`: some rollout has all 512 positions live.
All inputs are finite; a program needn't handle non-finite values. No bound on the sum of `tile_request_mask` on one device may be relied on, other than what follows from the above.
Results may differ from the reference program's by a relative error of at most 0.028.
Values may be sent and summed in bfloat16 or wider, within the bound.
A program may use at most 64 MiB of HBM per device.

```python
import jax
import jax.numpy as jnp
from jax import lax

MODEL_WIDTH = 8192
HEAD_SIZE = 128
HQ = 32
KEY_VALUE_HEADS = 4
ADAPTER_RANK = 64
PAGE = 4
TILE = 128
TOK_DEV = 64
SEQ = 512
ROLLOUTS = 4
GROUPS = 4
TILES = 4
PAGES_DEV = 16
PAGES = 128
N_CTX = 8
N_GRP = 4


def draw_queries(key, part):
    first = jax.random.fold_in(key, 0)
    output_shape = (ROLLOUTS, SEQ, HQ, HEAD_SIZE)
    value_rows = jnp.clip(jax.random.normal(first, output_shape, jnp.float32), -4.0, 4.0)
    return value_rows.reshape(ROLLOUTS, SEQ, HQ * HEAD_SIZE).astype(jnp.bfloat16)


def draw_lengths(key, part):
    first, second = jax.random.split(key)
    base = jax.random.randint(first, (ROLLOUTS,), SEQ // 4, SEQ + 1)
    chosen = jax.random.randint(second, (), 0, ROLLOUTS)
    return jnp.where(jnp.arange(ROLLOUTS) == chosen, SEQ, base).astype(jnp.int32)


def draw_page_lookup_table(key, part):
    ppd = TOK_DEV // PAGE
    most = max(2, (ppd + N_GRP - 1) // N_GRP)
    half_way = N_GRP // 2

    def row(sub, forced):
        k1, k2, k3, k4 = jax.random.split(sub, 4)
        order = jax.random.permutation(k1, N_GRP)
        where_half = jnp.argmax(order == half_way)
        swapped = order.at[where_half].set(order[0]).at[0].set(half_way)
        order = jnp.where(forced, swapped, order)
        rest = jnp.tile(order[1:], most)
        picked = rest[jax.random.permutation(k2, rest.shape[0])[:ppd - most]]
        offsets = jnp.concatenate([jnp.full((most,), order[0]), picked])
        offsets = offsets[jax.random.permutation(k3, ppd)]
        dest = (jnp.arange(N_GRP)[:, None] + offsets[None, :]) % N_GRP
        slots = jax.vmap(lambda kk: jax.random.permutation(kk, ppd))(jax.random.split(k4, N_GRP))
        slot = slots[dest, jnp.arange(ppd)[None, :]]
        return dest * ppd + slot
    table = jax.vmap(row)(jax.random.split(key, N_CTX), jnp.arange(N_CTX) == 0)
    return jnp.transpose(table, (1, 0, 2)).reshape(N_GRP, N_CTX * ppd).astype(jnp.int32)


def plant(values, own_key, least, high):
    index_at = [jax.random.randint(jax.random.fold_in(own_key, axis), (), 0, length) for axis, length in enumerate(values.shape)]
    main_axis = values.shape.index(max(values.shape))
    neighbour = index_at[:main_axis] + [(index_at[main_axis] + 1) % values.shape[main_axis]] + index_at[main_axis + 1:]
    return values.at[tuple(index_at)].set(least).at[tuple(neighbour)].set(high)


def steps_of(own_key, dims, pieces, smallest, top_value):
    factor_of = 1.0
    for position, blocks in pieces:
        steps = jax.random.uniform(jax.random.fold_in(jax.random.fold_in(own_key, 6), position), (blocks,), jnp.float32, smallest / len(pieces), top_value / len(pieces))
        factor_of = factor_of * jnp.repeat(jnp.exp(steps), dims[position] // blocks).reshape((-1,) + (1,) * (len(dims) - 1 - position))
    return factor_of


def scatter_about(own_key, extent, deviation, most, shards=(), held_as=jnp.bfloat16):
    factor_of = steps_of(own_key, extent, shards, -0.22, 0.18) if shards else 1.0
    result = jax.random.normal(own_key, extent, jnp.float32) * deviation * factor_of
    return jnp.minimum(jnp.maximum(result, -most), most).astype(held_as)


def setup_inputs(seed: int = 0) -> dict:
    splits = jax.random.split(jax.random.key(seed), 9)
    return {
        "tokens": scatter_about(splits[0], (ROLLOUTS, SEQ, MODEL_WIDTH), 1.0, 6.0, ((0, 4), (1, 8))),
        "queries": draw_queries(jax.random.fold_in(splits[8], 71), 0),
        "key_value_weight": scatter_about(splits[2], (MODEL_WIDTH, 2 * KEY_VALUE_HEADS * HEAD_SIZE), MODEL_WIDTH ** -0.5, 0.0625, ((0, 4),)),
        "adapter_down_weight": scatter_about(splits[3], (MODEL_WIDTH, 2 * ADAPTER_RANK), MODEL_WIDTH ** -0.5, 0.0625, ((0, 4),)),
        "adapter_up_weight": scatter_about(splits[4], (2, ADAPTER_RANK, KEY_VALUE_HEADS * HEAD_SIZE), ADAPTER_RANK ** -0.5, 0.75),
        "tile_request_mask": plant((jax.random.randint(splits[5], (ROLLOUTS, TILES, TILES), 0, 2) < 1).astype(jnp.int32), jax.random.fold_in(splits[5], 1), 0, 1),
        "lengths": draw_lengths(jax.random.fold_in(splits[8], 71), 0),
        "page_lookup_table": draw_page_lookup_table(jax.random.fold_in(splits[8], 71), 0),
    }


THETA = 500000.0
ADAPTER_SCALE = 0.5


def rotate(key_rows, token_positions):
    half_split = HEAD_SIZE // 2
    freq = THETA ** (-(2.0 * jnp.arange(half_split, dtype=jnp.float32)) / HEAD_SIZE)
    angle = token_positions.astype(jnp.float32)[:, None] * freq[None, :]
    cosine = jnp.cos(angle)[:, None, :]
    sine = jnp.sin(angle)[:, None, :]
    first = key_rows[..., :half_split]
    second = key_rows[..., half_split:]
    return jnp.concatenate([first * cosine - second * sine, second * cosine + first * sine], -1)


def project_inputs(hidden_input, key_value_weight, adapter_down_weight, adapter_up_weight, token_positions):
    column_width = MODEL_WIDTH // N_GRP
    column_span = key_value_weight.shape[1]

    def step(total, slot_index):
        xs = lax.dynamic_slice_in_dim(hidden_input, slot_index * column_width, column_width, 1)
        ws = lax.dynamic_slice_in_dim(key_value_weight, slot_index * column_width, column_width, 0)
        adapter_factor = lax.dynamic_slice_in_dim(adapter_down_weight, slot_index * column_width, column_width, 0)
        term = jnp.concatenate([jnp.dot(xs, ws, preferred_element_type=jnp.float32),
                                jnp.dot(xs, adapter_factor, preferred_element_type=jnp.float32)], 1)
        term = lax.optimization_barrier(term.astype(jnp.bfloat16)).astype(jnp.float32)
        return total + term, None

    start = jnp.zeros((hidden_input.shape[0], column_span + 2 * ADAPTER_RANK), jnp.float32)
    summed_output, _ = lax.scan(step, start, jnp.arange(N_GRP, dtype=jnp.int32))
    half_split = KEY_VALUE_HEADS * HEAD_SIZE
    low_rank_state = summed_output[:, column_span:].astype(jnp.bfloat16)
    key_rows = summed_output[:, :half_split] + ADAPTER_SCALE * jnp.dot(low_rank_state[:, :ADAPTER_RANK], adapter_up_weight[0], preferred_element_type=jnp.float32)
    value_rows = summed_output[:, half_split:column_span] + ADAPTER_SCALE * jnp.dot(low_rank_state[:, ADAPTER_RANK:], adapter_up_weight[1], preferred_element_type=jnp.float32)
    key_rows = rotate(key_rows.reshape(-1, KEY_VALUE_HEADS, HEAD_SIZE), token_positions).reshape(-1, half_split)
    return key_rows.astype(jnp.bfloat16), value_rows.astype(jnp.bfloat16)


def attend(queries, key_rows, value_rows, tile_request_mask, length):
    group = HQ // KEY_VALUE_HEADS
    qb = 512 if SEQ % 512 == 0 else SEQ
    key_f = key_rows.astype(jnp.float32).reshape(SEQ, KEY_VALUE_HEADS, HEAD_SIZE)
    val_f = value_rows.astype(jnp.float32).reshape(SEQ, KEY_VALUE_HEADS, HEAD_SIZE)
    kpos = jnp.arange(SEQ, dtype=jnp.int32)
    ktile = kpos // TILE
    tiles = jnp.arange(TILES, dtype=jnp.int32)
    tile_live = (tile_request_mask > 0) | (tiles[:, None] == tiles[None, :])
    scale = 1.0 / (HEAD_SIZE ** 0.5)

    def block(slot_index):
        start = slot_index * qb
        qs = lax.dynamic_slice_in_dim(queries, start, qb, 0).astype(jnp.float32).reshape(qb, KEY_VALUE_HEADS, group, HEAD_SIZE)
        qpos = start + jnp.arange(qb, dtype=jnp.int32)
        score = jnp.einsum('qhgd,khd->hgqk', qs, key_f) * scale
        live = tile_live[qpos // TILE][:, ktile]
        allowed = ((kpos[None, :] <= qpos[:, None]) & live & (kpos[None, :] < length)) | (kpos[None, :] == qpos[:, None])
        masked = jnp.where(allowed, score, -jnp.inf)
        peak = jnp.max(masked, axis=-1, keepdims=True)
        expo = jnp.where(allowed, jnp.exp(masked - peak), 0.0)
        total = jnp.sum(expo, axis=-1, keepdims=True)
        out = jnp.einsum('hgqk,khd->hgqd', expo, val_f) / total
        out = jnp.transpose(out, (2, 0, 1, 3)).reshape(qb, HQ * HEAD_SIZE)
        out = jnp.where((qpos < length)[:, None], out, 0.0)
        return out.astype(jnp.bfloat16)

    blocks = lax.map(block, jnp.arange(SEQ // qb, dtype=jnp.int32))
    return blocks.reshape(SEQ, HQ * HEAD_SIZE)


def reference(tokens, queries, key_value_weight, adapter_down_weight, adapter_up_weight, tile_request_mask, lengths, page_lookup_table):
    token_positions = jnp.arange(SEQ, dtype=jnp.int32)

    def one(slot_index):
        key_rows, value_rows = project_inputs(tokens[slot_index], key_value_weight, adapter_down_weight, adapter_up_weight, token_positions)
        out = attend(queries[slot_index], key_rows, value_rows, tile_request_mask[slot_index], lengths[slot_index])
        return out, jnp.concatenate([key_rows, value_rows], 1)

    attended, kv_all = lax.map(one, jnp.arange(ROLLOUTS, dtype=jnp.int32))
    column_width = kv_all.shape[2]
    pages = kv_all.reshape(ROLLOUTS, PAGES, PAGE, column_width)
    dest = (page_lookup_table // PAGES_DEV).astype(jnp.int32)
    slot = (page_lookup_table % PAGES_DEV).astype(jnp.int32)
    block_of = (jnp.arange(PAGES, dtype=jnp.int32) // PAGES_DEV)[None, :]
    target = (block_of * PAGES_DEV + slot).astype(jnp.int32)
    cache = jnp.zeros((GROUPS, PAGES, PAGE, column_width), jnp.bfloat16)
    cache = cache.at[dest, target].set(pages)
    return attended, cache
```

```python
import functools
import math

import jax
import jax.numpy as jnp
from jax import lax
from jax.experimental import pallas as pl
from jax.experimental.pallas import tpu as pltpu
from jax.sharding import PartitionSpec as P

HEAD_SIZE = 128
HQ = 32
KEY_VALUE_HEADS = 4
PAGE = 4
TILE = 128
THETA = 500000.0
ADAPTER_SCALE = 0.5
CHUNKS = 2
MESH = pl.DeviceIdType.MESH
F32 = jnp.float32
BF16 = jnp.bfloat16


def iota(shape, axis):
    return lax.broadcasted_iota(jnp.int32, shape, axis)


def page_rows(table, ppd):
    eye = iota((ppd, ppd), 0) == iota((ppd, ppd), 1)
    dest = lax.div(table, ppd)
    slot = lax.rem(table, ppd)
    wide = jnp.broadcast_to(dest.astype(F32), (ppd, ppd))
    column = jnp.sum(jnp.where(eye, wide, 0.0), axis=1, keepdims=True)
    same = wide == column
    lane_later = iota((ppd, ppd), 1) > iota((ppd, ppd), 0)
    lane_earlier = iota((ppd, ppd), 1) < iota((ppd, ppd), 0)
    order_row = jnp.sum(jnp.where(same & lane_later, 1.0, 0.0), axis=0, keepdims=True)
    order_col = jnp.sum(jnp.where(same & lane_earlier, 1.0, 0.0), axis=1, keepdims=True)
    return dest, slot, order_row, order_col


def kernel(
    groups, nz, ny,
    tokens, queries, kvw, dw, up, mask, lengths, table,
    att_out, cache_out,
    wbuf, qbuf, xbuf, part, rbuf, kv, pout, pin, pickp, placep, bias, cosb, sinb, mst, lst, acc,
    wsem, qsem, osem, xs, xr, rs, rr, zs, ys, ls, kr, ps, pr,
):
    me = lax.axis_index("grp")
    ctx = lax.axis_index("ctx")
    z = ctx // ny
    y = ctx % ny
    tok = qbuf.shape[0]
    ck = tok // CHUNKS
    width = xbuf.shape[3]
    cols = kvw.shape[1]
    half = cols // 2
    ppd = tok // PAGE
    most = max(2, -(-ppd // groups))
    rows = most * PAGE
    nctx = nz * ny
    per = HQ // KEY_VALUE_HEADS

    def partner(j):
        p = me
        for b in range(groups.bit_length()):
            if (j >> b) & 1:
                p = p + (1 << b) * (1 - 2 * ((me // (1 << b)) % 2))
        return p

    barrier = pltpu.get_barrier_semaphore()
    for j in range(1, groups):
        pl.semaphore_signal(barrier, inc=1, device_id={"grp": partner(j)}, device_id_type=MESH)
    for d in range(1, nz):
        pl.semaphore_signal(barrier, inc=1, device_id={"ctx": ((z + d) % nz) * ny + y}, device_id_type=MESH)
    for d in range(1, ny):
        pl.semaphore_signal(barrier, inc=1, device_id={"ctx": z * ny + (y + d) % ny}, device_id_type=MESH)

    wcopies = [
        pltpu.make_async_copy(kvw, wbuf.at[:, pl.ds(0, cols)], wsem.at[0]),
        pltpu.make_async_copy(dw, wbuf.at[:, pl.ds(cols, dw.shape[1])], wsem.at[1]),
    ]
    qcopy = pltpu.make_async_copy(queries.at[0], qbuf, qsem)
    ocopies = [
        pltpu.make_async_copy(
            tokens.at[0, pl.ds(c * ck, ck), pl.ds(pl.multiple_of(me * width, 128), width)],
            xbuf.at[c, 0], osem.at[c])
        for c in range(CHUNKS)
    ]

    def xcopy(c, j):
        other = partner(j)
        return pltpu.make_async_remote_copy(
            src_ref=tokens.at[0, pl.ds(c * ck, ck), pl.ds(pl.multiple_of(other * width, 128), width)],
            dst_ref=xbuf.at[c, j], send_sem=xs.at[c, j], recv_sem=xr.at[c, j],
            device_id={"grp": other}, device_id_type=MESH)

    def rcopy(c, j):
        return pltpu.make_async_remote_copy(
            src_ref=part.at[c, j], dst_ref=rbuf.at[c, j], send_sem=rs.at[c, j], recv_sem=rr.at[c, j],
            device_id={"grp": partner(j)}, device_id_type=MESH)

    def kcopy(c, source, target, send):
        return pltpu.make_async_remote_copy(
            src_ref=kv.at[c, source], dst_ref=kv.at[c, source], send_sem=send, recv_sem=kr.at[c, source],
            device_id={"ctx": target}, device_id_type=MESH)

    def pcopy(j):
        return pltpu.make_async_remote_copy(
            src_ref=pout.at[pl.ds(j * rows, rows)], dst_ref=pin.at[pl.ds(j * rows, rows)],
            send_sem=ps.at[j], recv_sem=pr.at[j],
            device_id={"grp": partner(j)}, device_id_type=MESH)

    pl.semaphore_wait(barrier, groups - 1 + nz - 1 + ny - 1)
    order = list(range(2, groups)) + [1]
    for c in range(CHUNKS):
        for j in order:
            xcopy(c, j).start()
    for copy in ocopies + wcopies + [qcopy]:
        copy.start()

    lane = iota((tok, HEAD_SIZE), 1)
    pair = lax.rem(lane, HEAD_SIZE // 2).astype(F32)
    freq = jnp.exp(pair * (-2.0 * math.log(THETA) / HEAD_SIZE))
    angle = (ctx * tok + iota((tok, HEAD_SIZE), 0)).astype(F32) * freq
    cosb[...] = jnp.cos(angle)
    sinb[...] = jnp.where(lane < HEAD_SIZE // 2, -1.0, 1.0) * jnp.sin(angle)

    length = lengths[0]
    qtile = (ctx * tok) // TILE
    n = nctx * ck
    for c in range(CHUNKS):
        lanes = iota((1, n), 1)
        kpos = lax.div(lanes, ck) * tok + c * ck + lax.rem(lanes, ck)
        ktile = lax.div(kpos, TILE)
        live = ktile == qtile
        for t in range(mask.shape[1]):
            live = live | ((ktile == t) & (mask[0, qtile, t] > 0))
        live = live & (kpos < length)
        qpos = ctx * tok + iota((tok, n), 0)
        later = jnp.broadcast_to(jnp.where(live, kpos, 1 << 30), (tok, n))
        same = jnp.broadcast_to(kpos, (tok, n)) == qpos
        bias[c] = jnp.where((later <= qpos) | same, 0.0, -1e30)

    @pl.loop(0, nctx)
    def _(s):
        @pl.when(s > ctx)
        def _():
            for c in range(CHUNKS):
                kv[c, s] = jnp.zeros((ck, cols), BF16)

    dest, slot, order_row, _ = page_rows(table[pl.ds(me, 1), :], ppd)
    r = iota((groups * rows, ppd), 0)
    target = lax.div(r, rows) ^ me
    nth = lax.div(lax.rem(r, rows), PAGE).astype(F32)
    chosen = jnp.where((jnp.broadcast_to(dest, r.shape) == target) & (order_row == nth), 1.0, 0.0)
    spread = jnp.where(lax.div(iota((ppd, tok), 1), PAGE) == iota((ppd, tok), 0), 1.0, 0.0)
    pick = jnp.dot(chosen.astype(BF16), spread.astype(BF16), preferred_element_type=F32)
    shape = (groups * rows, tok)
    line = lax.rem(iota(shape, 0), PAGE) == lax.rem(iota(shape, 1), PAGE)
    pickp[...] = jnp.where(line, pick, 0.0).astype(BF16)

    place = jnp.zeros((tok, groups * rows), F32)
    for j in range(groups):
        dest, slot, _, order_col = page_rows(table[pl.ds(partner(j), 1), :], ppd)
        o = lax.div(iota((tok, ppd), 0), PAGE)
        here = jnp.where((jnp.broadcast_to(slot, o.shape) == o) & (jnp.broadcast_to(dest, o.shape) == me), 1.0, 0.0)
        i = iota((ppd, groups * rows), 1)
        nth = lax.div(lax.rem(i, rows), PAGE).astype(F32)
        there = jnp.where((lax.div(i, rows) == j) & (order_col == nth), 1.0, 0.0)
        place = place + jnp.dot(here.astype(BF16), there.astype(BF16), preferred_element_type=F32)
    shape = (tok, groups * rows)
    line = lax.rem(iota(shape, 0), PAGE) == lax.rem(iota(shape, 1), PAGE)
    placep[...] = jnp.where(line, place, 0.0).astype(BF16)

    def project(c, first, last):
        x = xbuf[c, first:last].reshape((last - first) * ck, width)
        term = jnp.dot(x, wbuf[...], preferred_element_type=F32).astype(BF16)
        part[c, first:last] = term.reshape(last - first, ck, term.shape[1])
        for j in range(first, last):
            if j:
                rcopy(c, j).start()

    for copy in ocopies + wcopies:
        copy.wait()
    for c in range(CHUNKS):
        xcopy(c, 1).wait_recv()
        project(c, 0, 2)
    for c in range(CHUNKS):
        for j in range(2, groups):
            xcopy(c, j).wait_recv()
        project(c, 2, groups)

    for c in range(CHUNKS):
        total = part[c, 0].astype(F32)
        for j in range(1, groups):
            rcopy(c, j).wait_recv()
            total = total + rbuf[c, j].astype(F32)
        low = total[:, cols:].astype(BF16)
        first = iota(low.shape, 1) < low.shape[1] // 2
        none = jnp.zeros_like(low)
        keys = total[:, :half] + ADAPTER_SCALE * jnp.dot(
            jnp.where(first, low, none), up[...], preferred_element_type=F32)
        values = total[:, half:cols] + ADAPTER_SCALE * jnp.dot(
            jnp.where(first, none, low), up[...], preferred_element_type=F32)
        cosine = cosb[pl.ds(c * ck, ck), :]
        sine = sinb[pl.ds(c * ck, ck), :]
        for h in range(KEY_VALUE_HEADS):
            k = keys[:, h * HEAD_SIZE:(h + 1) * HEAD_SIZE]
            k = k * cosine + pltpu.roll(k, HEAD_SIZE // 2, 1) * sine
            kv[c, ctx, :, pl.ds(h * HEAD_SIZE, HEAD_SIZE)] = k.astype(BF16)
        kv[c, ctx, :, pl.ds(half, half)] = values.astype(BF16)
        for d in range(1, nz):
            @pl.when(z + d < nz)
            def _():
                kcopy(c, ctx, ctx + d * ny, zs.at[c, d]).start()
        for d in range(1, ny):
            @pl.when(y + d < ny)
            def _():
                kcopy(c, ctx, ctx + d, ys.at[c, d]).start()

    own = jnp.concatenate([kv[c, ctx] for c in range(CHUNKS)], axis=0)
    pout[...] = jnp.dot(pickp[...], own, preferred_element_type=F32).astype(BF16)
    for j in range(1, groups):
        pcopy(j).start()
    pin[pl.ds(0, rows), :] = pout[pl.ds(0, rows), :]
    qcopy.wait()

    scale = 1.0 / HEAD_SIZE**0.5
    for c in range(CHUNKS):
        for d in range(1, nz):
            @pl.when(d <= z)
            def _():
                source = ctx - d * ny
                kcopy(c, source, z * ny + (y + 1) % ny, ls.at[c, d, 1]).wait_recv()
                for e in range(1, ny):
                    kcopy(c, source, z * ny + (y + e) % ny, ls.at[c, d, e]).start()
        for d in range(1, ny):
            other = (y + d) % ny
            @pl.when(other < y)
            def _():
                kcopy(c, z * ny + other, z * ny + other, ys.at[c, d]).wait_recv()
            for e in range(1, nz):
                @pl.when(e <= z)
                def _():
                    kcopy(c, (z - e) * ny + other, z * ny + other, ls.at[c, e, d]).wait_recv()

        for h in range(KEY_VALUE_HEADS):
            q = jnp.concatenate(
                [qbuf[:, pl.ds((h * per + g) * HEAD_SIZE, HEAD_SIZE)] for g in range(per)], axis=0)
            k = kv[c, :, :, pl.ds(h * HEAD_SIZE, HEAD_SIZE)].reshape(n, HEAD_SIZE)
            v = kv[c, :, :, pl.ds(half + h * HEAD_SIZE, HEAD_SIZE)].reshape(n, HEAD_SIZE)
            s = lax.dot_general(q, k, (((1,), (1,)), ((), ())), preferred_element_type=F32) * scale
            s = (s.reshape(per, tok, n) + bias[c][None]).reshape(per * tok, n)
            peak = jnp.max(s, axis=1, keepdims=True)
            if c:
                before = mst[h]
                peak = jnp.maximum(peak, before)
            e = jnp.exp(s - peak)
            total = jnp.sum(e, axis=1, keepdims=True)
            out = jnp.dot(e.astype(BF16), v, preferred_element_type=F32)
            if c:
                factor = jnp.exp(before - peak)
                total = total + lst[h] * factor
                out = out + acc[h] * factor
            if c < CHUNKS - 1:
                mst[h] = peak
                lst[h] = total
                acc[h] = out
            else:
                out = out / total
                alive = ctx * tok + iota((tok, HEAD_SIZE), 0) < length
                for g in range(per):
                    piece = jnp.where(alive, out[g * tok:(g + 1) * tok], 0.0)
                    att_out[0, :, pl.ds((h * per + g) * HEAD_SIZE, HEAD_SIZE)] = piece.astype(BF16)
        if c == 0:
            for j in range(1, groups):
                pcopy(j).wait_recv()
            cache_out[...] = jnp.dot(placep[...], pin[...], preferred_element_type=F32).astype(BF16)

    for c in range(CHUNKS):
        for j in range(1, groups):
            xcopy(c, j).wait_send()
            rcopy(c, j).wait_send()
        for d in range(1, nz):
            @pl.when(z + d < nz)
            def _():
                kcopy(c, ctx, ctx + d * ny, zs.at[c, d]).wait_send()
            @pl.when(d <= z)
            def _():
                for e in range(1, ny):
                    kcopy(c, ctx - d * ny, z * ny + (y + e) % ny, ls.at[c, d, e]).wait_send()
        for d in range(1, ny):
            @pl.when(y + d < ny)
            def _():
                kcopy(c, ctx, ctx + d, ys.at[c, d]).wait_send()
    for j in range(1, groups):
        pcopy(j).wait_send()


def local(nctx, groups, tokens, queries, kvw, dw, up, mask, lengths, table):
    ny = 1
    while ny * ny * 4 <= nctx and nctx % (ny * 2) == 0:
        ny *= 2
    nz = nctx // ny
    tok = tokens.shape[1]
    ck = tok // CHUNKS
    width, cols = kvw.shape
    full = cols + dw.shape[1]
    ppd = tok // PAGE
    rows = max(2, -(-ppd // groups)) * PAGE
    per = HQ // KEY_VALUE_HEADS
    n = nctx * ck
    dma = pltpu.SemaphoreType.DMA
    hbm = pl.BlockSpec(memory_space=pl.ANY)
    vmem = pl.BlockSpec(memory_space=pltpu.VMEM)
    smem = pl.BlockSpec(memory_space=pltpu.SMEM)
    attended, cache = pl.pallas_call(
        functools.partial(kernel, groups, nz, ny),
        out_shape=(
            jax.ShapeDtypeStruct(queries.shape, BF16),
            jax.ShapeDtypeStruct((tok, cols), BF16),
        ),
        in_specs=[hbm, hbm, hbm, hbm, vmem, smem, smem, vmem],
        out_specs=(vmem, vmem),
        scratch_shapes=[
            pltpu.VMEM((width, full), BF16),
            pltpu.VMEM((tok, HQ * HEAD_SIZE), BF16),
            pltpu.VMEM((CHUNKS, groups, ck, width), BF16),
            pltpu.VMEM((CHUNKS, groups, ck, full), BF16),
            pltpu.VMEM((CHUNKS, groups, ck, full), BF16),
            pltpu.VMEM((CHUNKS, nctx, ck, cols), BF16),
            pltpu.VMEM((groups * rows, cols), BF16),
            pltpu.VMEM((groups * rows, cols), BF16),
            pltpu.VMEM((groups * rows, tok), BF16),
            pltpu.VMEM((tok, groups * rows), BF16),
            pltpu.VMEM((CHUNKS, tok, n), F32),
            pltpu.VMEM((tok, HEAD_SIZE), F32),
            pltpu.VMEM((tok, HEAD_SIZE), F32),
            pltpu.VMEM((KEY_VALUE_HEADS, per * tok, 1), F32),
            pltpu.VMEM((KEY_VALUE_HEADS, per * tok, 1), F32),
            pltpu.VMEM((KEY_VALUE_HEADS, per * tok, HEAD_SIZE), F32),
            dma((2,)),
            dma,
            dma((CHUNKS,)),
            dma((CHUNKS, groups)),
            dma((CHUNKS, groups)),
            dma((CHUNKS, groups)),
            dma((CHUNKS, groups)),
            dma((CHUNKS, nz)),
            dma((CHUNKS, ny)),
            dma((CHUNKS, nz, ny)),
            dma((CHUNKS, nctx)),
            dma((groups,)),
            dma((groups,)),
        ],
        compiler_params=pltpu.CompilerParams(
            collective_id=0, has_side_effects=True, vmem_limit_bytes=56 * 1024 * 1024
        ),
    )(tokens, queries, kvw, dw, up.reshape(-1, up.shape[2]), mask, lengths, table)
    return attended, cache.reshape(1, ppd, PAGE, cols)


def solution(mesh):
    in_specs = (
        P("grp", "ctx", None),
        P("grp", "ctx", None),
        P("grp", None),
        P("grp", None),
        P(),
        P("grp", None, None),
        P("grp"),
        P(None, "ctx"),
    )
    out_specs = (P("grp", "ctx", None), P("grp", "ctx", None, None))
    body = functools.partial(local, mesh.shape["ctx"], mesh.shape["grp"])
    return jax.shard_map(body, mesh=mesh, in_specs=in_specs, out_specs=out_specs, check_vma=False)
```

```python
import functools
import math

import jax
import jax.numpy as jnp
from jax import lax
from jax.experimental import pallas as pl
from jax.experimental.pallas import tpu as pltpu
from jax.sharding import PartitionSpec as P

HEAD_SIZE = 128
HQ = 32
KEY_VALUE_HEADS = 4
PAGE = 4
TILE = 128
THETA = 500000.0
ADAPTER_SCALE = 0.5
CHUNKS = 4
DEPTH = 2
SPANS = ((0, 3), (3, 4))
MESH = pl.DeviceIdType.MESH
F32 = jnp.float32
BF16 = jnp.bfloat16


def iota(shape, axis):
    return lax.broadcasted_iota(jnp.int32, shape, axis)


def page_rows(table, ppd):
    eye = iota((ppd, ppd), 0) == iota((ppd, ppd), 1)
    dest = lax.div(table, ppd)
    slot = lax.rem(table, ppd)
    wide = jnp.broadcast_to(dest.astype(F32), (ppd, ppd))
    column = jnp.sum(jnp.where(eye, wide, 0.0), axis=1, keepdims=True)
    same = wide == column
    lane_later = iota((ppd, ppd), 1) > iota((ppd, ppd), 0)
    lane_earlier = iota((ppd, ppd), 1) < iota((ppd, ppd), 0)
    order_row = jnp.sum(jnp.where(same & lane_later, 1.0, 0.0), axis=0, keepdims=True)
    order_col = jnp.sum(jnp.where(same & lane_earlier, 1.0, 0.0), axis=1, keepdims=True)
    return dest, slot, order_row, order_col


def kernel(
    groups, nz, ny,
    tokens, queries, kvw, dw, up, mask, lengths, table,
    att_out, cache_out,
    wbuf, qbuf, near, far, nearp, nearr, farp, cross, summed, farr, kv, pout, pin, pickp, placep, bias, cosb, sinb,
    mst, lst, acc,
    wsem, qsem, osem, ns, nr, ms, mr, xs, xr, cs, cr, rs, rr, zs, ys, ls, kr, ps, pr, ready,
):
    me = lax.axis_index("grp")
    ctx = lax.axis_index("ctx")
    z = ctx // ny
    y = ctx % ny
    tok = qbuf.shape[0]
    ck = tok // CHUNKS
    width = near.shape[2]
    pairs = groups // 2 - 1
    cols = kvw.shape[1]
    half = cols // 2
    ppd = tok // PAGE
    most = max(2, -(-ppd // groups))
    rows = most * PAGE
    nctx = nz * ny
    per = HQ // KEY_VALUE_HEADS

    def partner(j):
        p = me
        for b in range(groups.bit_length()):
            if (j >> b) & 1:
                p = p + (1 << b) * (1 - 2 * ((me // (1 << b)) % 2))
        return p

    barrier = pltpu.get_barrier_semaphore()
    for j in range(1, groups):
        pl.semaphore_signal(barrier, inc=1, device_id={"grp": partner(j)}, device_id_type=MESH)

    @pl.when(z > 0)
    def _():
        pl.semaphore_signal(barrier, inc=1, device_id={"ctx": ctx - ny}, device_id_type=MESH)

    @pl.when(z < nz - 1)
    def _():
        pl.semaphore_signal(barrier, inc=1, device_id={"ctx": ctx + ny}, device_id_type=MESH)

    for d in range(1, ny):
        pl.semaphore_signal(barrier, inc=1, device_id={"ctx": z * ny + (y + d) % ny}, device_id_type=MESH)

    wcopies = [
        pltpu.make_async_copy(kvw, wbuf.at[:, pl.ds(0, cols)], wsem.at[0]),
        pltpu.make_async_copy(dw, wbuf.at[:, pl.ds(cols, dw.shape[1])], wsem.at[1]),
    ]
    qcopy = pltpu.make_async_copy(queries.at[0], qbuf, qsem)
    ocopy = pltpu.make_async_copy(
        tokens.at[0, :, pl.ds(pl.multiple_of(me * width, 128), width)], near.at[0], osem)

    def ncopy():
        return pltpu.make_async_remote_copy(
            src_ref=tokens.at[0, :, pl.ds(pl.multiple_of(partner(1) * width, 128), width)],
            dst_ref=near.at[1], send_sem=ns, recv_sem=nr, device_id={"grp": partner(1)}, device_id_type=MESH)

    def mcopy():
        return pltpu.make_async_remote_copy(
            src_ref=nearp.at[1], dst_ref=nearr, send_sem=ms, recv_sem=mr,
            device_id={"grp": partner(1)}, device_id_type=MESH)

    def xcopy(c, j):
        other = partner(j)
        return pltpu.make_async_remote_copy(
            src_ref=tokens.at[0, pl.ds(c * ck, ck), pl.ds(pl.multiple_of(other * width, 128), width)],
            dst_ref=far.at[c, j - 2], send_sem=xs.at[c, j], recv_sem=xr.at[c, j],
            device_id={"grp": other}, device_id_type=MESH)

    def ccopy(c, k):
        return pltpu.make_async_remote_copy(
            src_ref=farp.at[c, 2 * k + 1], dst_ref=cross.at[c, k], send_sem=cs.at[c, k], recv_sem=cr.at[c, k],
            device_id={"grp": partner(1)}, device_id_type=MESH)

    def rcopy(c, k):
        return pltpu.make_async_remote_copy(
            src_ref=summed.at[c, k], dst_ref=farr.at[c, k], send_sem=rs.at[c, k], recv_sem=rr.at[c, k],
            device_id={"grp": partner(2 * k + 2)}, device_id_type=MESH)

    def kcopy(c, source, target, send):
        return pltpu.make_async_remote_copy(
            src_ref=kv.at[c, source], dst_ref=kv.at[c, source], send_sem=send, recv_sem=kr.at[c, source],
            device_id={"ctx": target}, device_id_type=MESH)

    def pcopy(j):
        return pltpu.make_async_remote_copy(
            src_ref=pout.at[pl.ds(j * rows, rows)], dst_ref=pin.at[pl.ds(j * rows, rows)],
            send_sem=ps.at[j], recv_sem=pr.at[j],
            device_id={"grp": partner(j)}, device_id_type=MESH)

    for copy in wcopies + [ocopy, qcopy]:
        copy.start()
    pl.semaphore_wait(barrier, groups - 1 + ny - 1 + jnp.where(z > 0, 1, 0) + jnp.where(z < nz - 1, 1, 0))
    for c in range(DEPTH):
        for j in range(2, groups):
            xcopy(c, j).start()
    ncopy().start()

    def tell_of(d):
        @pl.when((z > 0) & (z + d - 1 < nz))
        def _():
            pl.semaphore_signal(ready, inc=1, device_id={"ctx": ctx - ny}, device_id_type=MESH)

    tell_of(2)

    lane = iota((tok, HEAD_SIZE), 1)
    pair = lax.rem(lane, HEAD_SIZE // 2).astype(F32)
    freq = jnp.exp(pair * (-2.0 * math.log(THETA) / HEAD_SIZE))
    angle = (ctx * tok + iota((tok, HEAD_SIZE), 0)).astype(F32) * freq
    cosb[...] = jnp.cos(angle)
    sinb[...] = jnp.where(lane < HEAD_SIZE // 2, -1.0, 1.0) * jnp.sin(angle)

    length = lengths[0]
    qtile = (ctx * tok) // TILE
    n = nctx * ck
    for c in range(CHUNKS):
        lanes = iota((1, n), 1)
        kpos = lax.div(lanes, ck) * tok + c * ck + lax.rem(lanes, ck)
        ktile = lax.div(kpos, TILE)
        live = ktile == qtile
        for t in range(mask.shape[1]):
            live = live | ((ktile == t) & (mask[0, qtile, t] > 0))
        live = live & (kpos < length)
        qpos = ctx * tok + iota((tok, n), 0)
        later = jnp.broadcast_to(jnp.where(live, kpos, 1 << 30), (tok, n))
        same = jnp.broadcast_to(kpos, (tok, n)) == qpos
        bias[:, c * n:(c + 1) * n] = jnp.where((later <= qpos) | same, 0.0, -1e30)

    @pl.loop(0, nctx)
    def _(s):
        @pl.when(s > ctx)
        def _():
            for c in range(CHUNKS):
                kv[c, s] = jnp.zeros((ck, cols), BF16)

    for d in range(3, nz + 1):
        @pl.when(z + d - 1 < nz)
        def _():
            pl.semaphore_wait(ready, 1)
        tell_of(d)

    def page_tables():
        dest, slot, order_row, _ = page_rows(table[pl.ds(me, 1), :], ppd)
        r = iota((groups * rows, ppd), 0)
        target = lax.div(r, rows) ^ me
        nth = lax.div(lax.rem(r, rows), PAGE).astype(F32)
        chosen = jnp.where((jnp.broadcast_to(dest, r.shape) == target) & (order_row == nth), 1.0, 0.0)
        spread = jnp.where(lax.div(iota((ppd, tok), 1), PAGE) == iota((ppd, tok), 0), 1.0, 0.0)
        pick = jnp.dot(chosen.astype(BF16), spread.astype(BF16), preferred_element_type=F32)
        shape = (groups * rows, tok)
        line = lax.rem(iota(shape, 0), PAGE) == lax.rem(iota(shape, 1), PAGE)
        pickp[...] = jnp.where(line, pick, 0.0).astype(BF16)

        place = jnp.zeros((tok, groups * rows), F32)
        for j in range(groups):
            dest, slot, _, order_col = page_rows(table[pl.ds(partner(j), 1), :], ppd)
            o = lax.div(iota((tok, ppd), 0), PAGE)
            here = jnp.where((jnp.broadcast_to(slot, o.shape) == o) & (jnp.broadcast_to(dest, o.shape) == me), 1.0, 0.0)
            i = iota((ppd, groups * rows), 1)
            nth = lax.div(lax.rem(i, rows), PAGE).astype(F32)
            there = jnp.where((lax.div(i, rows) == j) & (order_col == nth), 1.0, 0.0)
            place = place + jnp.dot(here.astype(BF16), there.astype(BF16), preferred_element_type=F32)
        shape = (tok, groups * rows)
        line = lax.rem(iota(shape, 0), PAGE) == lax.rem(iota(shape, 1), PAGE)
        placep[...] = jnp.where(line, place, 0.0).astype(BF16)

    ocopy.wait()
    for copy in wcopies:
        copy.wait()
    ncopy().wait_recv()
    x = near[...].reshape(2 * tok, width)
    nearp[...] = jnp.dot(x, wbuf[...], preferred_element_type=F32).astype(BF16).reshape(nearp.shape)
    mcopy().start()

    def project(c):
        for j in range(2, groups):
            xcopy(c, j).wait_recv()
        if c + DEPTH < CHUNKS:
            for j in range(2, groups):
                xcopy(c, j).wait_send()
                xcopy(c + DEPTH, j).start()
        x = far[c].reshape(2 * pairs * ck, width)
        term = jnp.dot(x, wbuf[...], preferred_element_type=F32).astype(BF16)
        farp[c] = term.reshape(2 * pairs, ck, term.shape[1])
        for k in range(pairs):
            ccopy(c, k).start()

    def chip_sum(c):
        for k in range(pairs):
            ccopy(c, k).wait_recv()
            summed[c, k] = (farp[c, 2 * k].astype(F32) + cross[c, k].astype(F32)).astype(BF16)
            rcopy(c, k).start()

    def finish(c):
        if c == 0:
            mcopy().wait_recv()
        total = nearp[0, pl.ds(c * ck, ck), :].astype(F32) + nearr[pl.ds(c * ck, ck), :].astype(F32)
        for k in range(pairs):
            rcopy(c, k).wait_recv()
            total = total + farr[c, k].astype(F32)
        low = total[:, cols:].astype(BF16)
        first = iota(low.shape, 1) < low.shape[1] // 2
        none = jnp.zeros_like(low)
        keys = total[:, :half] + ADAPTER_SCALE * jnp.dot(
            jnp.where(first, low, none), up[...], preferred_element_type=F32)
        values = total[:, half:cols] + ADAPTER_SCALE * jnp.dot(
            jnp.where(first, none, low), up[...], preferred_element_type=F32)
        cosine = cosb[pl.ds(c * ck, ck), :]
        sine = sinb[pl.ds(c * ck, ck), :]
        for h in range(KEY_VALUE_HEADS):
            k = keys[:, h * HEAD_SIZE:(h + 1) * HEAD_SIZE]
            k = k * cosine + pltpu.roll(k, HEAD_SIZE // 2, 1) * sine
            kv[c, ctx, :, pl.ds(h * HEAD_SIZE, HEAD_SIZE)] = k.astype(BF16)
        kv[c, ctx, :, pl.ds(half, half)] = values.astype(BF16)
        for d in range(1, nz):
            @pl.when(z + d < nz)
            def _():
                kcopy(c, ctx, ctx + d * ny, zs.at[c, d]).start()
        for d in range(1, ny):
            @pl.when(y + d < ny)
            def _():
                kcopy(c, ctx, ctx + d, ys.at[c, d]).start()

    def relay(c):
        for d in range(1, nz):
            @pl.when(d <= z)
            def _():
                source = ctx - d * ny
                kcopy(c, source, z * ny + (y + 1) % ny, ls.at[c, d, 1]).wait_recv()
                for e in range(1, ny):
                    kcopy(c, source, z * ny + (y + e) % ny, ls.at[c, d, e]).start()

    def landed(c):
        for d in range(1, ny):
            other = (y + d) % ny
            @pl.when(other < y)
            def _():
                kcopy(c, z * ny + other, z * ny + other, ys.at[c, d]).wait_recv()
            for e in range(1, nz):
                @pl.when(e <= z)
                def _():
                    kcopy(c, (z - e) * ny + other, z * ny + other, ls.at[c, e, d]).wait_recv()

    def attend(i):
        first, last = SPANS[i]
        m = (last - first) * n
        for h in range(KEY_VALUE_HEADS):
            q = jnp.concatenate(
                [qbuf[:, pl.ds((h * per + g) * HEAD_SIZE, HEAD_SIZE)] for g in range(per)], axis=0)
            k = kv[first:last, :, :, pl.ds(h * HEAD_SIZE, HEAD_SIZE)].reshape(m, HEAD_SIZE)
            v = kv[first:last, :, :, pl.ds(half + h * HEAD_SIZE, HEAD_SIZE)].reshape(m, HEAD_SIZE)
            s = lax.dot_general(q, k, (((1,), (1,)), ((), ())), preferred_element_type=F32) * scale
            s = (s.reshape(per, tok, m) + bias[:, first * n:last * n][None]).reshape(per * tok, m)
            peak = jnp.max(s, axis=1, keepdims=True)
            if i:
                before = mst[h]
                peak = jnp.maximum(peak, before)
            e = jnp.exp(s - peak)
            total = jnp.sum(e, axis=1, keepdims=True)
            out = jnp.dot(e.astype(BF16), v, preferred_element_type=F32)
            if i:
                factor = jnp.exp(before - peak)
                total = total + lst[h] * factor
                out = out + acc[h] * factor
            if i < len(SPANS) - 1:
                mst[h] = peak
                lst[h] = total
                acc[h] = out
            else:
                out = out / total
                alive = ctx * tok + iota((tok, HEAD_SIZE), 0) < length
                for g in range(per):
                    piece = jnp.where(alive, out[g * tok:(g + 1) * tok], 0.0)
                    att_out[0, :, pl.ds((h * per + g) * HEAD_SIZE, HEAD_SIZE)] = piece.astype(BF16)
    length = lengths[0]
    scale = 1.0 / HEAD_SIZE**0.5
    page_tables()
    for c in range(CHUNKS):
        project(c)
        chip_sum(c)
        if c >= 1:
            finish(c - 1)
        if c >= 2:
            relay(c - 2)
    finish(CHUNKS - 1)

    own = jnp.concatenate([kv[c, ctx] for c in range(CHUNKS)], axis=0)
    pout[...] = jnp.dot(pickp[...], own, preferred_element_type=F32).astype(BF16)
    for j in range(1, groups):
        pcopy(j).start()
    pin[pl.ds(0, rows), :] = pout[pl.ds(0, rows), :]
    qcopy.wait()
    for c in range(CHUNKS - 2, SPANS[0][1]):
        relay(c)
    for i, (first, last) in enumerate(SPANS):
        if i == len(SPANS) - 1:
            for j in range(1, groups):
                pcopy(j).wait_recv()
            cache = jnp.dot(placep[...], pin[...], preferred_element_type=F32).astype(BF16)
            cache_out[0] = cache.reshape(cache_out.shape[1:])
        for c in range(max(first, CHUNKS - 2, SPANS[0][1]), last):
            relay(c)
        for c in range(first, last):
            landed(c)
        attend(i)

    for c in range(CHUNKS):
        for j in range(2, groups):
            if c + DEPTH >= CHUNKS:
                xcopy(c, j).wait_send()
        for k in range(pairs):
            ccopy(c, k).wait_send()
            rcopy(c, k).wait_send()
        for d in range(1, nz):
            @pl.when(z + d < nz)
            def _():
                kcopy(c, ctx, ctx + d * ny, zs.at[c, d]).wait_send()
            @pl.when(d <= z)
            def _():
                for e in range(1, ny):
                    kcopy(c, ctx - d * ny, z * ny + (y + e) % ny, ls.at[c, d, e]).wait_send()
        for d in range(1, ny):
            @pl.when(y + d < ny)
            def _():
                kcopy(c, ctx, ctx + d, ys.at[c, d]).wait_send()
    for j in range(1, groups):
        pcopy(j).wait_send()
    ncopy().wait_send()
    mcopy().wait_send()


def hand_over(attended, cache, attended_out, cache_out, first, second, sems):
    arrays = ((attended, first, attended_out), (cache, second, cache_out))
    into = [pltpu.make_async_copy(a, b, sems.at[0, i]) for i, (a, b, _) in enumerate(arrays)]
    back = [pltpu.make_async_copy(b, c, sems.at[1, i]) for i, (_, b, c) in enumerate(arrays)]
    for copy in into:
        copy.start()
    for a, b in zip(into, back):
        a.wait()
        b.start()
    for copy in back:
        copy.wait()


def local(nctx, groups, tokens, queries, kvw, dw, up, mask, lengths, table):
    ny = 1
    while ny * ny * 4 <= nctx and nctx % (ny * 2) == 0:
        ny *= 2
    nz = nctx // ny
    tok = tokens.shape[1]
    ck = tok // CHUNKS
    width, cols = kvw.shape
    full = cols + dw.shape[1]
    ppd = tok // PAGE
    rows = max(2, -(-ppd // groups)) * PAGE
    per = HQ // KEY_VALUE_HEADS
    n = nctx * ck
    pairs = groups // 2 - 1
    dma = pltpu.SemaphoreType.DMA
    hbm = pl.BlockSpec(memory_space=pl.ANY)
    vmem = pl.BlockSpec(memory_space=pltpu.VMEM)
    smem = pl.BlockSpec(memory_space=pltpu.SMEM)
    attended, cache = pl.pallas_call(
        functools.partial(kernel, groups, nz, ny),
        out_shape=(
            jax.ShapeDtypeStruct(queries.shape, BF16),
            jax.ShapeDtypeStruct((1, ppd, PAGE, cols), BF16),
        ),
        in_specs=[hbm, hbm, hbm, hbm, vmem, smem, smem, vmem],
        out_specs=(vmem, vmem),
        scratch_shapes=[
            pltpu.VMEM((width, full), BF16),
            pltpu.VMEM((tok, HQ * HEAD_SIZE), BF16),
            pltpu.VMEM((2, tok, width), BF16),
            pltpu.VMEM((CHUNKS, groups - 2, ck, width), BF16),
            pltpu.VMEM((2, tok, full), BF16),
            pltpu.VMEM((tok, full), BF16),
            pltpu.VMEM((CHUNKS, groups - 2, ck, full), BF16),
            pltpu.VMEM((CHUNKS, pairs, ck, full), BF16),
            pltpu.VMEM((CHUNKS, pairs, ck, full), BF16),
            pltpu.VMEM((CHUNKS, pairs, ck, full), BF16),
            pltpu.VMEM((CHUNKS, nctx, ck, cols), BF16),
            pltpu.VMEM((groups * rows, cols), BF16),
            pltpu.VMEM((groups * rows, cols), BF16),
            pltpu.VMEM((groups * rows, tok), BF16),
            pltpu.VMEM((tok, groups * rows), BF16),
            pltpu.VMEM((tok, CHUNKS * n), F32),
            pltpu.VMEM((tok, HEAD_SIZE), F32),
            pltpu.VMEM((tok, HEAD_SIZE), F32),
            pltpu.VMEM((KEY_VALUE_HEADS, per * tok, 1), F32),
            pltpu.VMEM((KEY_VALUE_HEADS, per * tok, 1), F32),
            pltpu.VMEM((KEY_VALUE_HEADS, per * tok, HEAD_SIZE), F32),
            dma((2,)),
            dma,
            dma,
            dma,
            dma,
            dma,
            dma,
            dma((CHUNKS, groups)),
            dma((CHUNKS, groups)),
            dma((CHUNKS, pairs)),
            dma((CHUNKS, pairs)),
            dma((CHUNKS, pairs)),
            dma((CHUNKS, pairs)),
            dma((CHUNKS, nz)),
            dma((CHUNKS, ny)),
            dma((CHUNKS, nz, ny)),
            dma((CHUNKS, nctx)),
            dma((groups,)),
            dma((groups,)),
            pltpu.SemaphoreType.REGULAR,
        ],
        compiler_params=pltpu.CompilerParams(
            collective_id=0, has_side_effects=True, vmem_limit_bytes=56 * 1024 * 1024
        ),
    )(tokens, queries, kvw, dw, up.reshape(-1, up.shape[2]), mask, lengths, table)
    return pl.pallas_call(
        hand_over,
        out_shape=(
            jax.ShapeDtypeStruct(attended.shape, BF16),
            jax.ShapeDtypeStruct(cache.shape, BF16),
        ),
        in_specs=[hbm, hbm],
        out_specs=(hbm, hbm),
        scratch_shapes=[pltpu.VMEM(attended.shape, BF16), pltpu.VMEM(cache.shape, BF16), dma((2, 2))],
    )(attended, cache)


def solution(mesh):
    in_specs = (
        P("grp", "ctx", None),
        P("grp", "ctx", None),
        P("grp", None),
        P("grp", None),
        P(),
        P("grp", None, None),
        P("grp"),
        P(None, "ctx"),
    )
    out_specs = (P("grp", "ctx", None), P("grp", "ctx", None, None))
    body = functools.partial(local, mesh.shape["ctx"], mesh.shape["grp"])
    return jax.shard_map(body, mesh=mesh, in_specs=in_specs, out_specs=out_specs, check_vma=False)
```
